128 devices in a mesh: stream: 16 (over z, y), passage: 4 (over x_hi, core), span: 2 (over x_lo).
Axes of the slice: x: 4 (x_hi: 2, x_lo: 2; x = x_hi * 2 + x_lo), y: 4, z: 4, core: 2. Of those that a mesh axis runs over, the one named last changes fastest.
Arguments:
- residual: float32 [6, 32, 256, 256], P(None, 'stream', 'passage', 'span'), may hold values from -4 to 4
- dq_old: float32 [6, 32, 256, 256], P(None, 'stream', 'passage', 'span'), may hold values from -6 to 6
- lateral_coef: float32 [32, 256, 256], P('stream', 'passage', 'span'), may hold values from 0.05 to 0.25
- diag_inverse: float32 [6, 6, 32, 256, 256], P(None, None, 'stream', 'passage', 'span'), may hold values from -1 to 1.2, as said below
- match_list: int32 [16, 256], P('stream', 'passage'), may hold values from 0 to 255, as said below
- slide_weight: float32 [256], P('passage'), may hold values from 0 to 1
Outputs:
- dq_new: float32 [6, 32, 256, 256], P(None, 'stream', 'passage', 'span')
The draws below stay inside these ranges and needn't reach their ends.
Inputs may be any that keep to these rules, and one draw needn't show every extreme that they name: match_list[b, p] = (p + offset_b) mod 256, where offset_b = (offset_0 + b * 64) mod 256. `diag_inverse`: each 6x6 block is a diagonal scaling of the identity plus a small antisymmetric part.
All inputs are finite; a program needn't handle non-finite values.
Results may differ from the reference program's by a relative error of at most 0.00013.
Values sent between devices are 32-bit elements; how exact they have to be, the bound alone decides.
No kernel may reach another device: no remote copies, remote signals or barrier semaphores. Data moves between devices by JAX's collectives and lax.ppermute only.
A program may use at most 320 MiB of HBM per device.

```python
import math
import jax
import jax.numpy as jnp
from jax import lax

UNKNOWNS_PER_BOX = 6
CP = 64
AXIAL_SECTIONS = 32
BLOCKS = 16
NP = 256
NZ = 256


def draw_diag_inverse(key, part):
    generator_seeds = jax.random.split(key, 7)
    decay_delay = jax.random.uniform(generator_seeds[0], (UNKNOWNS_PER_BOX,)) < 0.5
    slow_rate = jax.random.uniform(generator_seeds[1], (UNKNOWNS_PER_BOX,), minval=0.5, maxval=2.0) / AXIAL_SECTIONS
    fast_rate = jax.random.uniform(generator_seeds[2], (UNKNOWNS_PER_BOX,), minval=1.0 / 12.0, maxval=1.0 / 6.0)
    rate = jnp.where(decay_delay, slow_rate, fast_rate)[:, None, None, None]
    rough = jax.random.uniform(generator_seeds[3], (UNKNOWNS_PER_BOX, AXIAL_SECTIONS, NP, NZ), minval=0.5, maxval=1.5)
    correction_rounds = jax.random.randint(generator_seeds[4], (UNKNOWNS_PER_BOX, 3), 0, AXIAL_SECTIONS)
    pairing_counts_found = jnp.any(jnp.arange(AXIAL_SECTIONS)[None, None, :] == correction_rounds[:, :, None], axis=1)
    losses = jax.random.uniform(generator_seeds[5], (UNKNOWNS_PER_BOX, AXIAL_SECTIONS), minval=0.5, maxval=0.8)
    multiplier = jnp.where(pairing_counts_found, losses, 1.0)[:, :, None, None]
    scaling = jnp.exp(-rate * rough) * multiplier
    spread = jax.random.uniform(generator_seeds[6], (UNKNOWNS_PER_BOX, UNKNOWNS_PER_BOX, AXIAL_SECTIONS, NP, NZ), minval=-0.06, maxval=0.06)
    skewed = spread - jnp.swapaxes(spread, 0, 1)
    ident = (jnp.arange(UNKNOWNS_PER_BOX)[:, None] == jnp.arange(UNKNOWNS_PER_BOX)[None, :]).astype(jnp.float32)
    return (scaling[:, None] * (ident[:, :, None, None, None] + skewed)).astype(jnp.float32)


def draw_match_list(key, part):
    offset = jax.random.randint(key, (), 0, NP)
    offsets = (offset + jnp.arange(BLOCKS) * CP) % NP
    return ((jnp.arange(NP)[None, :] + offsets[:, None]) % NP).astype(jnp.int32)


def block_scale(key, dims, cuts, smallest, high):
    loudness = 1.0
    for dim, blocks in cuts:
        draws = jax.random.uniform(jax.random.fold_in(jax.random.fold_in(key, 6), dim), (blocks,), jnp.float32, smallest / len(cuts), high / len(cuts))
        loudness = loudness * jnp.repeat(jnp.exp(draws), dims[dim] // blocks).reshape((-1,) + (1,) * (len(dims) - 1 - dim))
    return loudness


def bell_draw(own_key, extent, scale, bound, pieces=(), dtype=jnp.bfloat16):
    entries = scale * jax.random.normal(own_key, extent, jnp.float32)
    if pieces:
        entries = entries * block_scale(own_key, extent, pieces, -0.22, 0.18)
    return jnp.clip(entries, -bound, bound).astype(dtype)


def setup_inputs(seed: int = 0) -> dict:
    streams_of = jax.random.split(jax.random.key(seed), 7)
    return {
        "residual": bell_draw(streams_of[0], (UNKNOWNS_PER_BOX, AXIAL_SECTIONS, NP, NZ), 0.3, 4.0, ((1, 16), (2, 4), (3, 2)), jnp.float32),
        "dq_old": bell_draw(streams_of[1], (UNKNOWNS_PER_BOX, AXIAL_SECTIONS, NP, NZ), 1.0, 6.0, ((1, 16), (2, 4), (3, 2)), jnp.float32),
        "lateral_coef": jnp.clip(jnp.exp(math.log(0.25) - 1.609438 * jax.random.uniform(streams_of[2], (AXIAL_SECTIONS, NP, NZ), jnp.float32) ** block_scale(streams_of[2], (AXIAL_SECTIONS, NP, NZ), ((0, 16), (1, 4), (2, 2)), -0.2, 0.2)), 0.05, 0.25),
        "diag_inverse": draw_diag_inverse(jax.random.fold_in(streams_of[6], 71), 0),
        "match_list": draw_match_list(jax.random.fold_in(streams_of[6], 71), 0),
        "slide_weight": jnp.clip(1.0 * jax.random.uniform(streams_of[5], (NP,), jnp.float32) ** block_scale(streams_of[5], (NP,), ((0, 4),), -0.2, 0.2), 0.0, 1.0),
    }


def apply_block(matrix, vector):
    return jnp.einsum("ab...,b...->a...", matrix, vector, precision=lax.Precision.HIGHEST)


def reference(residual, dq_old, lateral_coef, diag_inverse, match_list, slide_weight):
    planes = residual.shape[1]
    annulus = residual.shape[2]
    padded = jnp.pad(dq_old, ((0, 0), (0, 0), (0, 0), (1, 1)))
    neighbours = jnp.roll(dq_old, 1, axis=2) + jnp.roll(dq_old, -1, axis=2)
    neighbours = neighbours + padded[..., 2:] + padded[..., :-2]
    source = residual - lateral_coef[None] * neighbours
    block_count = match_list.shape[0]
    stride = planes // block_count
    donor_planes = ((jnp.arange(block_count) * stride - 1) % planes).astype(jnp.int32)
    donor = jnp.take(dq_old, donor_planes, axis=1)
    first_index = match_list.astype(jnp.int32)[None, :, :, None]
    next_index = ((match_list + 1) % annulus).astype(jnp.int32)[None, :, :, None]
    weight = slide_weight[None, None, :, None]
    term = (1.0 - weight) * jnp.take_along_axis(donor, first_index, axis=2) + weight * jnp.take_along_axis(donor, next_index, axis=2)
    source = source.at[:, ::stride].add(term)
    matrices = jnp.moveaxis(diag_inverse, 2, 0)
    sources = jnp.moveaxis(source, 1, 0)

    def forward_solve_move(current, input_arrays):
        inverse, given = input_arrays
        current = apply_block(inverse, given + current)
        return current, current

    _, lowers = lax.scan(forward_solve_move, jnp.zeros_like(sources[0]), (matrices, sources))

    def upward_sweep_step(current, input_arrays):
        inverse, lowered = input_arrays
        current = lowered + apply_block(inverse, current)
        return current, current

    _, uppers = lax.scan(upward_sweep_step, jnp.zeros_like(sources[0]), (matrices, lowers), reverse=True)
    return jnp.moveaxis(uppers, 0, 1)
```

```python
import jax
import jax.numpy as jnp
from jax import lax
from jax.experimental import pallas as pl
from jax.experimental.pallas import tpu as pltpu
from jax.sharding import PartitionSpec as P

VARS = 6
PAIRS = [(a, b) for a in range(VARS) for b in range(a + 1, VARS)]
COEFS = VARS + len(PAIRS) + 1
PLANES = 2
SENT = PLANES * COEFS + PLANES * VARS + VARS
LANES = 128
PART = 4


def vmem():
    return pl.BlockSpec(memory_space=pltpu.VMEM)


def edges_kernel(dq_ref, rows_ref, cols_ref):
    span = lax.axis_index("span")
    height = dq_ref.shape[2]
    sub = lax.broadcasted_iota(jnp.int32, (8, LANES), 0)
    lane = lax.broadcasted_iota(jnp.int32, (height, LANES), 1)
    cols = jnp.zeros((height, LANES), jnp.float32)
    for v in range(VARS):
        rows_ref[v, 0:height] = dq_ref[v, 1]
        rows_ref[v, height : height + 8] = jnp.where(
            sub < 4, dq_ref[v, 0, 0:8], dq_ref[v, 0, height - 8 : height]
        )
        for p in range(PLANES):
            i = v * PLANES + p
            shift = lax.rem(i + 129 - 2 * span, 128)
            there = lax.rem(i + 127 * span, 128)
            cols = jnp.where(lane == there, pltpu.roll(dq_ref[v, p], shift, 1), cols)
    cols_ref[...] = cols


def pack_kernel(d_ref, out_ref):
    tiles = d_ref.shape[3] // 8
    for p in range(PLANES):
        for t in range(tiles):
            d = [[d_ref[a, b, p, 8 * t : 8 * t + 8] for b in range(VARS)] for a in range(VARS)]
            s = [d[a][a] for a in range(VARS)]
            size = [jnp.abs(x) for x in s]
            inv = [jnp.where(x == 0.0, 0.0, 1.0 / x) for x in s]
            off_row = off_none = off_col = jnp.zeros_like(s[0])
            for a, b in PAIRS:
                off_row += jnp.abs(d[a][b] * s[b] + d[b][a] * s[a])
                off_none += jnp.abs(d[a][b] + d[b][a])
                off_col += jnp.abs(d[a][b] * s[a] + d[b][a] * s[b])
            is_row = (off_row <= off_none) & (off_row <= off_col)
            is_none = off_none <= off_col
            form = jnp.where(is_row, 0.0, jnp.where(is_none, 1.0, 2.0))
            values = list(s)
            for a, b in PAIRS:
                larger = size[a] >= size[b]
                row = jnp.where(larger, d[a][b] * inv[a], -d[b][a] * inv[b])
                col = jnp.where(larger, -d[b][a] * inv[a], d[a][b] * inv[b])
                values.append(jnp.where(is_row, row, jnp.where(is_none, d[a][b], col)))
            values.append(form)
            for i, value in enumerate(values):
                out_ref[2 * t, p * COEFS + i] = value[0:PART]
                out_ref[2 * t + 1, p * COEFS + i] = value[PART:8]


def source_kernel(
    match_ref, dq_ref, res_ref, coef_ref, weight_ref, core_ref, far_ref, cross_ref, cols_ref, _, out_ref, src, ring, sem
):
    q, span = lax.axis_index("passage"), lax.axis_index("span")
    height = dq_ref.shape[2]
    start = lax.rem(match_ref[0, 0] + 64, 256)
    tile, offset = start // 64, lax.rem(start, 64)
    odd = lax.rem(q, 2) == 1
    sub = lax.broadcasted_iota(jnp.int32, (height, LANES), 0)
    lane = lax.broadcasted_iota(jnp.int32, (height, LANES), 1)
    edge = lane == jnp.where(span == 0, LANES - 1, 0)
    weight = jnp.broadcast_to(weight_ref[...], (LANES, height)).T

    def pick(index, v, rows):
        way = jnp.bitwise_xor(index, q)
        near = jnp.where(way == 0, dq_ref[v, 1, 0:rows], core_ref[v, 0:rows])
        away = jnp.where(way == 2, far_ref[v, 0:rows], cross_ref[v, 0:rows])
        return jnp.where(way < 2, near, away)

    def put(index, value):
        for t in range(height // PART):
            src[t, index] = value[PART * t : PART * t + PART]

    for v in range(VARS):
        ring[v, 0:height] = pick(tile, v, height)
        ring[v, height : 2 * height] = pick(lax.rem(tile + 1, 4), v, height)
        for p in range(PLANES):
            x = dq_ref[v, p]
            if p == 1:
                last, first = height - 1, 0
            else:
                last, first = height + 7, height
            above = jnp.where(odd, core_ref[v, last : last + 1], cross_ref[v, last : last + 1])
            below = jnp.where(odd, cross_ref[v, first : first + 1], core_ref[v, first : first + 1])
            up = jnp.where(sub == 0, above, pltpu.roll(x, 1, 0))
            down = jnp.where(sub == height - 1, below, pltpu.roll(x, height - 1, 0))
            i = v * PLANES + p
            side = pltpu.roll(cols_ref[...], (LANES - i) % LANES, 1)
            left = jnp.where(lane == 0, 0.0, pltpu.roll(x, 1, 1))
            right = jnp.where(lane == LANES - 1, 0.0, pltpu.roll(x, LANES - 1, 1))
            near = up + down + (left + right + jnp.where(edge, side, 0.0))
            put(p * VARS + v, res_ref[v, p] - coef_ref[p] * near)
    for v in range(VARS):
        here = ring[v, pl.ds(offset, height)]
        after = ring[v, pl.ds(offset + 1, height)]
        put(PLANES * VARS + v, (1.0 - weight) * here + weight * after)
    copy = pltpu.make_async_copy(src, out_ref.at[:, PLANES * COEFS :], sem)
    copy.start()
    copy.wait()


def sweep_kernel(in_ref, out_ref):
    blocks = in_ref.shape[0]

    def block_of(b, p):
        base = p * COEFS
        s = [in_ref[b, base + a] for a in range(VARS)]
        k = {pair: in_ref[b, base + VARS + i] for i, pair in enumerate(PAIRS)}
        form = in_ref[b, base + COEFS - 1]
        return s, k, form == 0.0, form == 2.0

    def apply(block, x):
        s, k, is_row, is_col = block
        g = [jnp.where(is_col, s[b] * x[b], x[b]) for b in range(VARS)]
        out = []
        for a in range(VARS):
            terms = [k[a, b] * g[b] if a < b else k[b, a] * g[b] for b in range(VARS) if b != a]
            signs = [a < b for b in range(VARS) if b != a]
            plus = [t for t, up in zip(terms, signs) if up]
            minus = [t for t, up in zip(terms, signs) if not up]
            rest = tree(plus) - tree(minus) if plus and minus else (tree(plus) if plus else -tree(minus))
            out.append(s[a] * x[a] + jnp.where(is_row, s[a] * rest, rest))
        return out

    def tree(terms):
        while len(terms) > 1:
            terms = [sum(terms[i : i + 2][1:], terms[i]) for i in range(0, len(terms), 2)]
        return terms[0]

    def lower(b, x):
        before = lax.rem(b + blocks - 1, blocks)
        for p in range(PLANES):
            given = [in_ref[b, PLANES * COEFS + p * VARS + v] for v in range(VARS)]
            if p == 0:
                given = [given[v] + in_ref[before, PLANES * COEFS + PLANES * VARS + v] for v in range(VARS)]
            x = apply(block_of(b, p), [given[v] + x[v] for v in range(VARS)])
            for v in range(VARS):
                out_ref[b, v * PLANES + p] = x[v]
        return x

    def upper(i, x):
        b = blocks - 1 - i
        for p in reversed(range(PLANES)):
            y = apply(block_of(b, p), x)
            x = [out_ref[b, v * PLANES + p] + y[v] for v in range(VARS)]
            for v in range(VARS):
                out_ref[b, v * PLANES + p] = x[v]
        return x

    zero = [jnp.zeros((PART, LANES), jnp.float32) for _ in range(VARS)]
    lax.fori_loop(0, blocks, lower, zero, unroll=2)
    lax.fori_loop(0, blocks, upper, zero, unroll=2)


def unpack_kernel(in_ref, out_ref):
    for v in range(VARS):
        for p in range(PLANES):
            for t in range(in_ref.shape[0]):
                out_ref[v, p, PART * t : PART * t + PART] = in_ref[t, v * PLANES + p]


def on_device(residual, dq_old, lateral_coef, diag_inverse, match_list, slide_weight):
    height = residual.shape[2]
    blocks = lax.axis_size("stream")
    f32 = jnp.float32
    grant = pltpu.CompilerParams(vmem_limit_bytes=24 * 1024 * 1024)
    rows, cols = pl.pallas_call(
        edges_kernel,
        out_shape=(
            jax.ShapeDtypeStruct((VARS, height + 8, LANES), f32),
            jax.ShapeDtypeStruct((height, LANES), f32),
        ),
        in_specs=[vmem()],
        out_specs=(vmem(), vmem()),
        compiler_params=grant,
        name="edges",
    )(dq_old)
    far = lax.ppermute(rows, "passage", [(q, q ^ 2) for q in range(4)])
    cols = lax.ppermute(cols, "span", [(0, 1), (1, 0)])
    core = lax.ppermute(rows, "passage", [(q, q ^ 1) for q in range(4)])
    steps = 4
    packed = pl.pallas_call(
        pack_kernel,
        out_shape=jax.ShapeDtypeStruct((blocks, SENT, PART, LANES), f32),
        grid=(steps,),
        in_specs=[
            pl.BlockSpec((VARS, VARS, PLANES, height // steps, LANES), lambda i: (0, 0, 0, i, 0))
        ],
        out_specs=pl.BlockSpec((blocks // steps, PLANES * COEFS, PART, LANES), lambda i: (i, 0, 0, 0)),
        compiler_params=grant,
        name="pack",
    )(diag_inverse)
    cross = lax.ppermute(far, "passage", [(q, q ^ 1) for q in range(4)])
    any_space = pl.BlockSpec(memory_space=pl.ANY)
    sent = pl.pallas_call(
        source_kernel,
        out_shape=jax.ShapeDtypeStruct((blocks, SENT, PART, LANES), f32),
        in_specs=[pl.BlockSpec(memory_space=pltpu.SMEM)] + [vmem()] * 8 + [any_space],
        out_specs=any_space,
        scratch_shapes=[
            pltpu.VMEM((blocks, PLANES * VARS + VARS, PART, LANES), f32),
            pltpu.VMEM((VARS, 2 * height + 8, LANES), f32),
            pltpu.SemaphoreType.DMA,
        ],
        input_output_aliases={9: 0},
        compiler_params=grant,
        name="source",
    )(match_list, dq_old, residual, lateral_coef, slide_weight[None], core, far, cross, cols, packed)
    got = lax.all_to_all(sent, "stream", 0, 0)
    swept = pl.pallas_call(
        sweep_kernel,
        out_shape=jax.ShapeDtypeStruct((blocks, PLANES * VARS, PART, LANES), f32),
        in_specs=[vmem()],
        out_specs=vmem(),
        compiler_params=grant,
        name="sweep",
    )(got)
    back = lax.all_to_all(swept, "stream", 0, 0)
    return pl.pallas_call(
        unpack_kernel,
        out_shape=jax.ShapeDtypeStruct((VARS, PLANES, height, LANES), f32),
        in_specs=[vmem()],
        out_specs=vmem(),
        compiler_params=grant,
        name="unpack",
    )(back)


def solution(mesh):
    placed = (
        P(None, "stream", "passage", "span"),
        P(None, "stream", "passage", "span"),
        P("stream", "passage", "span"),
        P(None, None, "stream", "passage", "span"),
        P("stream", "passage"),
        P("passage"),
    )
    return jax.shard_map(
        on_device,
        mesh=mesh,
        in_specs=placed,
        out_specs=P(None, "stream", "passage", "span"),
        check_vma=False,
    )
```

```python
import jax
import jax.numpy as jnp
from jax import lax
from jax.experimental import pallas as pl
from jax.experimental.pallas import tpu as pltpu
from jax.sharding import PartitionSpec as P

VARS = 6
PAIRS = [(a, b) for a in range(VARS) for b in range(a + 1, VARS)]
COEFS = VARS + len(PAIRS)
PLANES = 2
FORM = PLANES * COEFS
SOURCE = FORM + 1
TERM = SOURCE + PLANES * VARS
SENT = TERM + VARS
LANES = 128
PART = 4


def vmem():
    return pl.BlockSpec(memory_space=pltpu.VMEM)


def edges_kernel(dq_ref, rows_ref, cols_ref, first, sems):
    span = lax.axis_index("span")
    height = first.shape[1]
    copies = [
        pltpu.make_async_copy(dq_ref.at[:, 1], rows_ref.at[:, 0:height], sems.at[0]),
        pltpu.make_async_copy(dq_ref.at[:, 0], first, sems.at[1]),
    ]
    for copy in copies:
        copy.start()
    for copy in copies:
        copy.wait()
    sub = lax.broadcasted_iota(jnp.int32, (8, LANES), 0)
    lane = lax.broadcasted_iota(jnp.int32, (height, LANES), 1)
    cols = jnp.zeros((height, LANES), jnp.float32)
    for v in range(VARS):
        rows_ref[v, height : height + 8] = jnp.where(
            sub < 4, first[v, 0:8], first[v, height - 8 : height]
        )
        for p in range(PLANES):
            i = v * PLANES + p
            shift = lax.rem(i + 129 - 2 * span, 128)
            there = lax.rem(i + 127 * span, 128)
            plane = rows_ref[v, 0:height] if p else first[v]
            cols = jnp.where(lane == there, pltpu.roll(plane, shift, 1), cols)
    cols_ref[...] = cols


def pack_kernel(d_ref, out_ref):
    def put(t, index, value):
        out_ref[2 * t, index] = value[0:PART]
        out_ref[2 * t + 1, index] = value[PART:8]

    for t in range(d_ref.shape[3] // 8):
        blocks = [
            [[d_ref[a, b, p, 8 * t : 8 * t + 8] for b in range(VARS)] for a in range(VARS)]
            for p in range(PLANES)
        ]
        off_row = off_none = off_col = jnp.zeros((8, LANES), jnp.float32)
        for d in blocks:
            for a, b in PAIRS:
                off_row += jnp.abs(d[a][b] * d[b][b] + d[b][a] * d[a][a])
                off_none += jnp.abs(d[a][b] + d[b][a])
                off_col += jnp.abs(d[a][b] * d[a][a] + d[b][a] * d[b][b])
        is_row = (off_row <= off_none) & (off_row <= off_col)
        is_none = off_none <= off_col
        put(t, FORM, jnp.where(is_row, 0.0, jnp.where(is_none, 1.0, 2.0)))
        for p, d in enumerate(blocks):
            s = [d[a][a] for a in range(VARS)]
            size = [jnp.abs(x) for x in s]
            inv = [jnp.where(x == 0.0, 0.0, 1.0 / x) for x in s]
            for a in range(VARS):
                put(t, p * COEFS + a, s[a])
            for i, (a, b) in enumerate(PAIRS):
                larger = size[a] >= size[b]
                row = jnp.where(larger, d[a][b] * inv[a], -d[b][a] * inv[b])
                col = jnp.where(larger, -d[b][a] * inv[a], d[a][b] * inv[b])
                value = jnp.where(is_row, row, jnp.where(is_none, d[a][b], col))
                put(t, p * COEFS + VARS + i, value)


def source_kernel(
    match_ref, dq_ref, res_ref, coef_ref, weight_ref, core_ref, far_ref, cross_ref, cols_ref, _, out_ref, src, ring, sem
):
    q, span = lax.axis_index("passage"), lax.axis_index("span")
    height = dq_ref.shape[2]
    start = lax.rem(match_ref[0, 0] + 64, 256)
    tile, offset = start // 64, lax.rem(start, 64)
    odd = lax.rem(q, 2) == 1
    sub = lax.broadcasted_iota(jnp.int32, (height, LANES), 0)
    lane = lax.broadcasted_iota(jnp.int32, (height, LANES), 1)
    edge = lane == jnp.where(span == 0, LANES - 1, 0)
    weight = jnp.broadcast_to(weight_ref[...], (LANES, height)).T

    def pick(index, v, rows):
        way = jnp.bitwise_xor(index, q)
        near = jnp.where(way == 0, dq_ref[v, 1, 0:rows], core_ref[v, 0:rows])
        away = jnp.where(way == 2, far_ref[v, 0:rows], cross_ref[v, 0:rows])
        return jnp.where(way < 2, near, away)

    def put(index, value):
        for t in range(height // PART):
            src[t, index] = value[PART * t : PART * t + PART]

    for v in range(VARS):
        ring[v, 0:height] = pick(tile, v, height)
        ring[v, height : 2 * height] = pick(lax.rem(tile + 1, 4), v, height)
        for p in range(PLANES):
            x = dq_ref[v, p]
            if p == 1:
                last, first = height - 1, 0
            else:
                last, first = height + 7, height
            above = jnp.where(odd, core_ref[v, last : last + 1], cross_ref[v, last : last + 1])
            below = jnp.where(odd, cross_ref[v, first : first + 1], core_ref[v, first : first + 1])
            up = jnp.where(sub == 0, above, pltpu.roll(x, 1, 0))
            down = jnp.where(sub == height - 1, below, pltpu.roll(x, height - 1, 0))
            i = v * PLANES + p
            side = pltpu.roll(cols_ref[...], (LANES - i) % LANES, 1)
            left = jnp.where(lane == 0, 0.0, pltpu.roll(x, 1, 1))
            right = jnp.where(lane == LANES - 1, 0.0, pltpu.roll(x, LANES - 1, 1))
            near = up + down + (left + right + jnp.where(edge, side, 0.0))
            put(p * VARS + v, res_ref[v, p] - coef_ref[p] * near)
    for v in range(VARS):
        here = ring[v, pl.ds(offset, height)]
        after = ring[v, pl.ds(offset + 1, height)]
        put(PLANES * VARS + v, (1.0 - weight) * here + weight * after)
    copy = pltpu.make_async_copy(src, out_ref.at[:, SOURCE:], sem)
    copy.start()
    copy.wait()


def sweep_kernel(in_ref, out_ref):
    blocks = in_ref.shape[0]

    def block_of(b, p):
        base = p * COEFS
        s = [in_ref[b, base + a] for a in range(VARS)]
        k = {pair: in_ref[b, base + VARS + i] for i, pair in enumerate(PAIRS)}
        form = in_ref[b, FORM]
        return s, k, form == 0.0, form == 2.0

    def apply(block, x):
        s, k, is_row, is_col = block
        g = [jnp.where(is_col, s[b] * x[b], x[b]) for b in range(VARS)]
        out = []
        for a in range(VARS):
            terms = [k[a, b] * g[b] if a < b else k[b, a] * g[b] for b in range(VARS) if b != a]
            signs = [a < b for b in range(VARS) if b != a]
            plus = [t for t, up in zip(terms, signs) if up]
            minus = [t for t, up in zip(terms, signs) if not up]
            rest = tree(plus) - tree(minus) if plus and minus else (tree(plus) if plus else -tree(minus))
            out.append(s[a] * x[a] + jnp.where(is_row, s[a] * rest, rest))
        return out

    def tree(terms):
        while len(terms) > 1:
            terms = [sum(terms[i : i + 2][1:], terms[i]) for i in range(0, len(terms), 2)]
        return terms[0]

    def lower(b, x):
        before = lax.rem(b + blocks - 1, blocks)
        for p in range(PLANES):
            given = [in_ref[b, SOURCE + p * VARS + v] for v in range(VARS)]
            if p == 0:
                given = [given[v] + in_ref[before, TERM + v] for v in range(VARS)]
            x = apply(block_of(b, p), [given[v] + x[v] for v in range(VARS)])
            for v in range(VARS):
                out_ref[b, v * PLANES + p] = x[v]
        return x

    def upper(i, x):
        b = blocks - 1 - i
        for p in reversed(range(PLANES)):
            y = apply(block_of(b, p), x)
            x = [out_ref[b, v * PLANES + p] + y[v] for v in range(VARS)]
            for v in range(VARS):
                out_ref[b, v * PLANES + p] = x[v]
        return x

    zero = [jnp.zeros((PART, LANES), jnp.float32) for _ in range(VARS)]
    lax.fori_loop(0, blocks, lower, zero, unroll=2)
    lax.fori_loop(0, blocks, upper, zero, unroll=2)


def unpack_kernel(in_ref, out_ref):
    for v in range(VARS):
        for p in range(PLANES):
            for t in range(in_ref.shape[0]):
                out_ref[v, p, PART * t : PART * t + PART] = in_ref[t, v * PLANES + p]


def on_device(residual, dq_old, lateral_coef, diag_inverse, match_list, slide_weight):
    height = residual.shape[2]
    blocks = lax.axis_size("stream")
    f32 = jnp.float32
    grant = pltpu.CompilerParams(vmem_limit_bytes=24 * 1024 * 1024)
    rows, cols = pl.pallas_call(
        edges_kernel,
        out_shape=(
            jax.ShapeDtypeStruct((VARS, height + 8, LANES), f32),
            jax.ShapeDtypeStruct((height, LANES), f32),
        ),
        in_specs=[pl.BlockSpec(memory_space=pltpu.HBM)],
        out_specs=(vmem(), vmem()),
        scratch_shapes=[
            pltpu.VMEM((VARS, height, LANES), f32),
            pltpu.SemaphoreType.DMA((2,)),
        ],
        compiler_params=grant,
        name="edges",
    )(dq_old)
    far = lax.ppermute(rows, "passage", [(q, q ^ 2) for q in range(4)])
    cols = lax.ppermute(cols, "span", [(0, 1), (1, 0)])
    core = lax.ppermute(rows, "passage", [(q, q ^ 1) for q in range(4)])
    steps = 4
    diag_inverse, rows = lax.optimization_barrier((diag_inverse, rows))
    packed = pl.pallas_call(
        pack_kernel,
        out_shape=jax.ShapeDtypeStruct((blocks, SENT, PART, LANES), f32),
        grid=(steps,),
        in_specs=[
            pl.BlockSpec((VARS, VARS, PLANES, height // steps, LANES), lambda i: (0, 0, 0, i, 0))
        ],
        out_specs=pl.BlockSpec((blocks // steps, SOURCE, PART, LANES), lambda i: (i, 0, 0, 0)),
        compiler_params=grant,
        name="pack",
    )(diag_inverse)
    far, core, cols, packed = lax.optimization_barrier((far, core, cols, packed))
    cross = lax.ppermute(far, "passage", [(q, q ^ 1) for q in range(4)])
    any_space = pl.BlockSpec(memory_space=pl.ANY)
    sent = pl.pallas_call(
        source_kernel,
        out_shape=jax.ShapeDtypeStruct((blocks, SENT, PART, LANES), f32),
        in_specs=[pl.BlockSpec(memory_space=pltpu.SMEM)] + [vmem()] * 8 + [any_space],
        out_specs=any_space,
        scratch_shapes=[
            pltpu.VMEM((blocks, PLANES * VARS + VARS, PART, LANES), f32),
            pltpu.VMEM((VARS, 2 * height + 8, LANES), f32),
            pltpu.SemaphoreType.DMA,
        ],
        input_output_aliases={9: 0},
        compiler_params=grant,
        name="source",
    )(match_list, dq_old, residual, lateral_coef, slide_weight[None], core, far, cross, cols, packed)
    got = lax.all_to_all(sent, "stream", 0, 0)
    swept = pl.pallas_call(
        sweep_kernel,
        out_shape=jax.ShapeDtypeStruct((blocks, PLANES * VARS, PART, LANES), f32),
        in_specs=[vmem()],
        out_specs=vmem(),
        compiler_params=grant,
        name="sweep",
    )(got)
    back = lax.all_to_all(swept, "stream", 0, 0)
    return pl.pallas_call(
        unpack_kernel,
        out_shape=jax.ShapeDtypeStruct((VARS, PLANES, height, LANES), f32),
        in_specs=[vmem()],
        out_specs=vmem(),
        compiler_params=grant,
        name="unpack",
    )(back)


def solution(mesh):
    placed = (
        P(None, "stream", "passage", "span"),
        P(None, "stream", "passage", "span"),
        P("stream", "passage", "span"),
        P(None, None, "stream", "passage", "span"),
        P("stream", "passage"),
        P("passage"),
    )
    return jax.shard_map(
        on_device,
        mesh=mesh,
        in_specs=placed,
        out_specs=P(None, "stream", "passage", "span"),
        check_vma=False,
    )
```

```python
import jax
import jax.numpy as jnp
from jax import lax
from jax.experimental import pallas as pl
from jax.experimental.pallas import tpu as pltpu
from jax.sharding import PartitionSpec as P

VARS = 6
PAIRS = [(a, b) for a in range(VARS) for b in range(a + 1, VARS)]
COEFS = VARS + len(PAIRS)
PLANES = 2
FORM = PLANES * COEFS
SOURCE = FORM + 1
TERM = SOURCE + PLANES * VARS
SENT = TERM + VARS
LANES = 128
PART = 4
EDGE_ROWS = 16


def vmem():
    return pl.BlockSpec(memory_space=pltpu.VMEM)


def edges_kernel(dq_ref, rows_ref):
    height = dq_ref.shape[2]
    for v in range(VARS):
        rows_ref[height * v : height * (v + 1)] = dq_ref[v, 1]
    edge = height * VARS
    rows_ref[edge:] = jnp.zeros((EDGE_ROWS, LANES), jnp.float32)
    for v in range(VARS):
        rows_ref[edge + 2 * v : edge + 2 * v + 1] = dq_ref[v, 0, 0:1]
        rows_ref[edge + 2 * v + 1 : edge + 2 * v + 2] = dq_ref[v, 0, height - 1 : height]


def columns_kernel(dq_ref, cols_ref):
    span = lax.axis_index("span")
    height = dq_ref.shape[2]
    lane = lax.broadcasted_iota(jnp.int32, (height, LANES), 1)
    cols = jnp.zeros((height, LANES), jnp.float32)
    for i in range(VARS * PLANES):
        shift = i + 2 - 2 * span
        plane = dq_ref[i // PLANES, i % PLANES]
        cols = jnp.where(lane == i + 1 - span, pltpu.roll(plane, shift, 1), cols)
    cols_ref[...] = cols.T[0:16]


def pack_kernel(d_ref, out_ref):
    def put(t, index, value):
        out_ref[2 * t, index] = value[0:PART]
        out_ref[2 * t + 1, index] = value[PART:8]

    for t in range(d_ref.shape[3] // 8):
        blocks = [
            [[d_ref[a, b, p, 8 * t : 8 * t + 8] for b in range(VARS)] for a in range(VARS)]
            for p in range(PLANES)
        ]
        off_row = off_none = off_col = jnp.zeros((8, LANES), jnp.float32)
        for d in blocks:
            for a, b in PAIRS:
                off_row += jnp.abs(d[a][b] * d[b][b] + d[b][a] * d[a][a])
                off_none += jnp.abs(d[a][b] + d[b][a])
                off_col += jnp.abs(d[a][b] * d[a][a] + d[b][a] * d[b][b])
        is_row = (off_row <= off_none) & (off_row <= off_col)
        is_none = off_none <= off_col
        put(t, FORM, jnp.where(is_row, 0.0, jnp.where(is_none, 1.0, 2.0)))
        for p, d in enumerate(blocks):
            s = [d[a][a] for a in range(VARS)]
            size = [jnp.abs(x) for x in s]
            inv = [jnp.where(x == 0.0, 0.0, 1.0 / x) for x in s]
            for a in range(VARS):
                put(t, p * COEFS + a, s[a])
            for i, (a, b) in enumerate(PAIRS):
                larger = size[a] >= size[b]
                row = jnp.where(larger, d[a][b] * inv[a], -d[b][a] * inv[b])
                col = jnp.where(larger, -d[b][a] * inv[a], d[a][b] * inv[b])
                value = jnp.where(is_row, row, jnp.where(is_none, d[a][b], col))
                put(t, p * COEFS + VARS + i, value)


def local_kernel(dq_ref, res_ref, coef_ref, core_ref, out_ref):
    odd = lax.rem(lax.axis_index("passage"), 2) == 1
    height = dq_ref.shape[2]
    sub = lax.broadcasted_iota(jnp.int32, (height, LANES), 0)
    lane = lax.broadcasted_iota(jnp.int32, (height, LANES), 1)
    for v in range(VARS):
        for p in range(PLANES):
            x = dq_ref[v, p]
            last, first = edge_rows(v, p, height)
            above = jnp.where(odd, core_ref[last : last + 1], 0.0)
            below = jnp.where(odd, 0.0, core_ref[first : first + 1])
            up = jnp.where(sub == 0, above, pltpu.roll(x, 1, 0))
            down = jnp.where(sub == height - 1, below, pltpu.roll(x, height - 1, 0))
            left = jnp.where(lane == 0, 0.0, pltpu.roll(x, 1, 1))
            right = jnp.where(lane == LANES - 1, 0.0, pltpu.roll(x, LANES - 1, 1))
            out_ref[v, p] = res_ref[v, p] - coef_ref[p] * (up + down + (left + right))


def edge_rows(v, plane, height):
    if plane:
        return height * (v + 1) - 1, height * v
    return height * VARS + 2 * v + 1, height * VARS + 2 * v


def source_kernel(
    match_ref, dq_ref, local_ref, coef_ref, weight_ref, core_ref, far_ref, cross_ref, cols_ref, _, out_ref, src, ring, sems
):
    q, span = lax.axis_index("passage"), lax.axis_index("span")
    height = dq_ref.shape[2]
    start = lax.rem(match_ref[0, 0] + 64, 256)
    tile, offset = start // 64, lax.rem(start, 64)
    odd = lax.rem(q, 2) == 1
    sub = lax.broadcasted_iota(jnp.int32, (height, LANES), 0)
    lane = lax.broadcasted_iota(jnp.int32, (height, LANES), 1)
    beyond = sub == jnp.where(odd, height - 1, 0)
    edge = lane == jnp.where(span == 0, LANES - 1, 0)
    weight = jnp.broadcast_to(weight_ref[...], (LANES, height)).T
    cols = jnp.concatenate([cols_ref[...], jnp.zeros((LANES - 16, height), jnp.float32)], 0).T

    def pick(index, v):
        way = jnp.bitwise_xor(index, q)
        face = slice(height * v, height * (v + 1))
        near = jnp.where(way == 0, dq_ref[v, 1], core_ref[face])
        away = jnp.where(way == 2, far_ref[face], cross_ref[face])
        return jnp.where(way < 2, near, away)

    def put(index, value):
        for t in range(height // PART):
            src[t, index] = value[PART * t : PART * t + PART]

    for v in range(VARS):
        for p in range(PLANES):
            last, first = edge_rows(v, p, height)
            row = jnp.where(odd, cross_ref[first : first + 1], cross_ref[last : last + 1])
            i = v * PLANES + p
            side = pltpu.roll(cols, LANES - 1 - i, 1)
            rest = jnp.where(beyond, row, 0.0) + jnp.where(edge, side, 0.0)
            put(p * VARS + v, local_ref[v, p] - coef_ref[p] * rest)
    width = PLANES * VARS
    copies = [
        pltpu.make_async_copy(src.at[:, 0:width], out_ref.at[:, SOURCE:TERM], sems.at[0]),
        pltpu.make_async_copy(src.at[:, width:], out_ref.at[:, TERM:], sems.at[1]),
    ]
    copies[0].start()
    for v in range(VARS):
        ring[v, 0:height] = pick(tile, v)
        ring[v, height : 2 * height] = pick(lax.rem(tile + 1, 4), v)
    for v in range(VARS):
        here = ring[v, pl.ds(offset, height)]
        after = ring[v, pl.ds(offset + 1, height)]
        put(width + v, (1.0 - weight) * here + weight * after)
    copies[1].start()
    for copy in copies:
        copy.wait()


def sweep_kernel(in_ref, out_ref):
    blocks = in_ref.shape[0]

    def block_of(b, p):
        base = p * COEFS
        s = [in_ref[b, base + a] for a in range(VARS)]
        k = {pair: in_ref[b, base + VARS + i] for i, pair in enumerate(PAIRS)}
        form = in_ref[b, FORM]
        return s, k, form == 0.0, form == 2.0

    def apply(block, x):
        s, k, is_row, is_col = block
        g = [jnp.where(is_col, s[b] * x[b], x[b]) for b in range(VARS)]
        out = []
        for a in range(VARS):
            terms = [k[a, b] * g[b] if a < b else k[b, a] * g[b] for b in range(VARS) if b != a]
            signs = [a < b for b in range(VARS) if b != a]
            plus = [t for t, up in zip(terms, signs) if up]
            minus = [t for t, up in zip(terms, signs) if not up]
            rest = tree(plus) - tree(minus) if plus and minus else (tree(plus) if plus else -tree(minus))
            out.append(s[a] * x[a] + jnp.where(is_row, s[a] * rest, rest))
        return out

    def tree(terms):
        while len(terms) > 1:
            terms = [sum(terms[i : i + 2][1:], terms[i]) for i in range(0, len(terms), 2)]
        return terms[0]

    def lower(b, x):
        before = lax.rem(b + blocks - 1, blocks)
        for p in range(PLANES):
            given = [in_ref[b, SOURCE + p * VARS + v] for v in range(VARS)]
            if p == 0:
                given = [given[v] + in_ref[before, TERM + v] for v in range(VARS)]
            x = apply(block_of(b, p), [given[v] + x[v] for v in range(VARS)])
            for v in range(VARS):
                out_ref[b, v * PLANES + p] = x[v]
        return x

    def upper(i, x):
        b = blocks - 1 - i
        for p in reversed(range(PLANES)):
            y = apply(block_of(b, p), x)
            x = [out_ref[b, v * PLANES + p] + y[v] for v in range(VARS)]
            for v in range(VARS):
                out_ref[b, v * PLANES + p] = x[v]
        return x

    zero = [jnp.zeros((PART, LANES), jnp.float32) for _ in range(VARS)]
    lax.fori_loop(0, blocks, lower, zero, unroll=2)
    lax.fori_loop(0, blocks, upper, zero, unroll=2)


def unpack_kernel(in_ref, out_ref):
    for v in range(VARS):
        for p in range(PLANES):
            for t in range(in_ref.shape[0]):
                out_ref[v, p, PART * t : PART * t + PART] = in_ref[t, v * PLANES + p]


def on_device(residual, dq_old, lateral_coef, diag_inverse, match_list, slide_weight):
    height = residual.shape[2]
    blocks = lax.axis_size("stream")
    f32 = jnp.float32
    grant = pltpu.CompilerParams(vmem_limit_bytes=24 * 1024 * 1024)
    rows = pl.pallas_call(
        edges_kernel,
        out_shape=jax.ShapeDtypeStruct((VARS * height + EDGE_ROWS, LANES), f32),
        in_specs=[vmem()],
        out_specs=vmem(),
        compiler_params=grant,
        name="edges",
    )(dq_old)
    cols = pl.pallas_call(
        columns_kernel,
        out_shape=jax.ShapeDtypeStruct((16, height), f32),
        in_specs=[vmem()],
        out_specs=vmem(),
        compiler_params=grant,
        name="columns",
    )(dq_old)
    far = lax.ppermute(rows, "passage", [(q, q ^ 2) for q in range(4)])
    cols = lax.ppermute(cols, "span", [(0, 1), (1, 0)])
    steps = 4
    packed = pl.pallas_call(
        pack_kernel,
        out_shape=jax.ShapeDtypeStruct((blocks, SENT, PART, LANES), f32),
        grid=(steps,),
        in_specs=[
            pl.BlockSpec((VARS, VARS, PLANES, height // steps, LANES), lambda i: (0, 0, 0, i, 0))
        ],
        out_specs=pl.BlockSpec((blocks // steps, SOURCE, PART, LANES), lambda i: (i, 0, 0, 0)),
        compiler_params=grant,
        name="pack",
    )(diag_inverse)
    core = lax.ppermute(rows, "passage", [(q, q ^ 1) for q in range(4)])
    local = pl.pallas_call(
        local_kernel,
        out_shape=jax.ShapeDtypeStruct((VARS, PLANES, height, LANES), f32),
        in_specs=[vmem()] * 4,
        out_specs=vmem(),
        compiler_params=grant,
        name="local",
    )(dq_old, residual, lateral_coef, core)
    cross = lax.ppermute(far, "passage", [(q, q ^ 1) for q in range(4)])
    any_space = pl.BlockSpec(memory_space=pl.ANY)
    sent = pl.pallas_call(
        source_kernel,
        out_shape=jax.ShapeDtypeStruct((blocks, SENT, PART, LANES), f32),
        in_specs=[pl.BlockSpec(memory_space=pltpu.SMEM)] + [vmem()] * 8 + [any_space],
        out_specs=any_space,
        scratch_shapes=[
            pltpu.VMEM((blocks, PLANES * VARS + VARS, PART, LANES), f32),
            pltpu.VMEM((VARS, 2 * height + 8, LANES), f32),
            pltpu.SemaphoreType.DMA((2,)),
        ],
        input_output_aliases={9: 0},
        compiler_params=grant,
        name="source",
    )(match_list, dq_old, local, lateral_coef, slide_weight[None], core, far, cross, cols, packed)
    got = lax.all_to_all(sent, "stream", 0, 0)
    swept = pl.pallas_call(
        sweep_kernel,
        out_shape=jax.ShapeDtypeStruct((blocks, PLANES * VARS, PART, LANES), f32),
        in_specs=[vmem()],
        out_specs=vmem(),
        compiler_params=grant,
        name="sweep",
    )(got)
    back = lax.all_to_all(swept, "stream", 0, 0)
    return pl.pallas_call(
        unpack_kernel,
        out_shape=jax.ShapeDtypeStruct((VARS, PLANES, height, LANES), f32),
        in_specs=[vmem()],
        out_specs=vmem(),
        compiler_params=grant,
        name="unpack",
    )(back)


def solution(mesh):
    placed = (
        P(None, "stream", "passage", "span"),
        P(None, "stream", "passage", "span"),
        P("stream", "passage", "span"),
        P(None, None, "stream", "passage", "span"),
        P("stream", "passage"),
        P("passage"),
    )
    return jax.shard_map(
        on_device,
        mesh=mesh,
        in_specs=placed,
        out_specs=P(None, "stream", "passage", "span"),
        check_vma=False,
    )
```

```python
import jax
import jax.numpy as jnp
from jax import lax
from jax.experimental import pallas as pl
from jax.experimental.pallas import tpu as pltpu
from jax.sharding import PartitionSpec as P

VARS = 6
PAIRS = [(a, b) for a in range(VARS) for b in range(a + 1, VARS)]
COEFS = VARS + len(PAIRS)
PLANES = 2
FORM = PLANES * COEFS
SOURCE = FORM + 1
TERM = SOURCE + PLANES * VARS
SENT = TERM + VARS
LANES = 128
PART = 4
EDGE_ROWS = 16


def vmem():
    return pl.BlockSpec(memory_space=pltpu.VMEM)


def edges_kernel(dq_ref, rows_ref):
    height = dq_ref.shape[2]
    for v in range(VARS):
        rows_ref[height * v : height * (v + 1)] = dq_ref[v, 1]
    edge = height * VARS
    rows_ref[edge:] = jnp.zeros((EDGE_ROWS, LANES), jnp.float32)
    for v in range(VARS):
        rows_ref[edge + 2 * v : edge + 2 * v + 1] = dq_ref[v, 0, 0:1]
        rows_ref[edge + 2 * v + 1 : edge + 2 * v + 2] = dq_ref[v, 0, height - 1 : height]


def columns_kernel(dq_ref, cols_ref):
    span = lax.axis_index("span")
    height = dq_ref.shape[2]
    lane = lax.broadcasted_iota(jnp.int32, (height, LANES), 1)
    cols = jnp.zeros((height, LANES), jnp.float32)
    for i in range(VARS * PLANES):
        shift = i + 2 - 2 * span
        plane = dq_ref[i // PLANES, i % PLANES]
        cols = jnp.where(lane == i + 1 - span, pltpu.roll(plane, shift, 1), cols)
    cols_ref[...] = cols.T[0:16]


def pack_kernel(d_ref, out_ref):
    def put(t, index, value):
        out_ref[2 * t, index] = value[0:PART]
        out_ref[2 * t + 1, index] = value[PART:8]

    for t in range(d_ref.shape[3] // 8):
        blocks = [
            [[d_ref[a, b, p, 8 * t : 8 * t + 8] for b in range(VARS)] for a in range(VARS)]
            for p in range(PLANES)
        ]
        off_row = off_none = off_col = jnp.zeros((8, LANES), jnp.float32)
        for d in blocks:
            for a, b in PAIRS:
                off_row += jnp.abs(d[a][b] * d[b][b] + d[b][a] * d[a][a])
                off_none += jnp.abs(d[a][b] + d[b][a])
                off_col += jnp.abs(d[a][b] * d[a][a] + d[b][a] * d[b][b])
        is_row = (off_row <= off_none) & (off_row <= off_col)
        is_none = off_none <= off_col
        put(t, FORM, jnp.where(is_row, 0.0, jnp.where(is_none, 1.0, 2.0)))
        for p, d in enumerate(blocks):
            s = [d[a][a] for a in range(VARS)]
            size = [jnp.abs(x) for x in s]
            inv = [jnp.where(x == 0.0, 0.0, 1.0 / x) for x in s]
            for a in range(VARS):
                put(t, p * COEFS + a, s[a])
            for i, (a, b) in enumerate(PAIRS):
                larger = size[a] >= size[b]
                row = jnp.where(larger, d[a][b] * inv[a], -d[b][a] * inv[b])
                col = jnp.where(larger, -d[b][a] * inv[a], d[a][b] * inv[b])
                value = jnp.where(is_row, row, jnp.where(is_none, d[a][b], col))
                put(t, p * COEFS + VARS + i, value)


def local_kernel(dq_ref, res_ref, coef_ref, core_ref, out_ref):
    odd = lax.rem(lax.axis_index("passage"), 2) == 1
    height = dq_ref.shape[2]
    sub = lax.broadcasted_iota(jnp.int32, (height, LANES), 0)
    lane = lax.broadcasted_iota(jnp.int32, (height, LANES), 1)
    for v in range(VARS):
        for p in range(PLANES):
            x = dq_ref[v, p]
            last, first = edge_rows(v, p, height)
            above = jnp.where(odd, core_ref[last : last + 1], 0.0)
            below = jnp.where(odd, 0.0, core_ref[first : first + 1])
            up = jnp.where(sub == 0, above, pltpu.roll(x, 1, 0))
            down = jnp.where(sub == height - 1, below, pltpu.roll(x, height - 1, 0))
            left = jnp.where(lane == 0, 0.0, pltpu.roll(x, 1, 1))
            right = jnp.where(lane == LANES - 1, 0.0, pltpu.roll(x, LANES - 1, 1))
            out_ref[v, p] = res_ref[v, p] - coef_ref[p] * (up + down + (left + right))


def edge_rows(v, plane, height):
    if plane:
        return height * (v + 1) - 1, height * v
    return height * VARS + 2 * v + 1, height * VARS + 2 * v


def source_kernel(
    match_ref, dq_ref, local_ref, coef_ref, weight_ref, core_ref, far_ref, cross_ref, cols_ref, _, out_ref, ring
):
    q, span = lax.axis_index("passage"), lax.axis_index("span")
    height = dq_ref.shape[2]
    start = lax.rem(match_ref[0, 0] + 64, 256)
    tile, offset = start // 64, lax.rem(start, 64)
    odd = lax.rem(q, 2) == 1
    sub = lax.broadcasted_iota(jnp.int32, (height, LANES), 0)
    lane = lax.broadcasted_iota(jnp.int32, (height, LANES), 1)
    beyond = sub == jnp.where(odd, height - 1, 0)
    edge = lane == jnp.where(span == 0, LANES - 1, 0)
    weight = jnp.broadcast_to(weight_ref[...], (LANES, height)).T
    cols = jnp.concatenate([cols_ref[...], jnp.zeros((LANES - 16, height), jnp.float32)], 0).T

    def pick(index, v):
        way = jnp.bitwise_xor(index, q)
        face = slice(height * v, height * (v + 1))
        near = jnp.where(way == 0, dq_ref[v, 1], core_ref[face])
        away = jnp.where(way == 2, far_ref[face], cross_ref[face])
        return jnp.where(way < 2, near, away)

    def put(index, value):
        for t in range(height // PART):
            out_ref[t, index] = value[PART * t : PART * t + PART]

    for v in range(VARS):
        for p in range(PLANES):
            last, first = edge_rows(v, p, height)
            row = jnp.where(odd, cross_ref[first : first + 1], cross_ref[last : last + 1])
            i = v * PLANES + p
            side = pltpu.roll(cols, LANES - 1 - i, 1)
            rest = jnp.where(beyond, row, 0.0) + jnp.where(edge, side, 0.0)
            put(SOURCE + p * VARS + v, local_ref[v, p] - coef_ref[p] * rest)
    for v in range(VARS):
        ring[v, 0:height] = pick(tile, v)
        ring[v, height : 2 * height] = pick(lax.rem(tile + 1, 4), v)
    for v in range(VARS):
        here = ring[v, pl.ds(offset, height)]
        after = ring[v, pl.ds(offset + 1, height)]
        put(TERM + v, (1.0 - weight) * here + weight * after)


def sweep_kernel(in_ref, out_ref):
    blocks = in_ref.shape[0]

    def block_of(b, p):
        base = p * COEFS
        s = [in_ref[b, base + a] for a in range(VARS)]
        k = {pair: in_ref[b, base + VARS + i] for i, pair in enumerate(PAIRS)}
        form = in_ref[b, FORM]
        is_row, is_col = form == 0.0, form == 2.0
        rows = [jnp.where(is_row, x, 1.0) for x in s]
        columns = [jnp.where(is_col, x, 1.0) for x in s]
        return s, k, rows, columns

    def apply(block, x):
        s, k, rows, columns = block
        g = [columns[b] * x[b] for b in range(VARS)]
        out = []
        for a in range(VARS):
            plus = tree([k[a, b] * g[b] for b in range(a + 1, VARS)])
            minus = tree([k[b, a] * g[b] for b in range(a)])
            rest = minus if plus is None else plus if minus is None else plus - minus
            out.append(s[a] * x[a] + rows[a] * (-rest if plus is None else rest))
        return out

    def tree(terms):
        while len(terms) > 1:
            terms = [sum(terms[i : i + 2][1:], terms[i]) for i in range(0, len(terms), 2)]
        return terms[0] if terms else None

    def lower(b, x):
        before = lax.rem(b + blocks - 1, blocks)
        for p in range(PLANES):
            given = [in_ref[b, SOURCE + p * VARS + v] for v in range(VARS)]
            if p == 0:
                given = [given[v] + in_ref[before, TERM + v] for v in range(VARS)]
            x = apply(block_of(b, p), [given[v] + x[v] for v in range(VARS)])
            for v in range(VARS):
                out_ref[b, v * PLANES + p] = x[v]
        return x

    def upper(i, x):
        b = blocks - 1 - i
        for p in reversed(range(PLANES)):
            y = apply(block_of(b, p), x)
            x = [out_ref[b, v * PLANES + p] + y[v] for v in range(VARS)]
            for v in range(VARS):
                out_ref[b, v * PLANES + p] = x[v]
        return x

    zero = [jnp.zeros((PART, LANES), jnp.float32) for _ in range(VARS)]
    lax.fori_loop(0, blocks, lower, zero, unroll=16)
    lax.fori_loop(0, blocks, upper, zero, unroll=16)


def unpack_kernel(in_ref, out_ref, held, sems):
    copies = []
    for v in range(VARS):
        for p in range(PLANES):
            for t in range(in_ref.shape[0]):
                held[v, p, PART * t : PART * t + PART] = in_ref[t, v * PLANES + p]
        copies.append(pltpu.make_async_copy(held.at[v], out_ref.at[v], sems.at[v]))
        copies[v].start()
    for copy in copies:
        copy.wait()


def on_device(residual, dq_old, lateral_coef, diag_inverse, match_list, slide_weight):
    height = residual.shape[2]
    blocks = lax.axis_size("stream")
    f32 = jnp.float32
    grant = pltpu.CompilerParams(vmem_limit_bytes=24 * 1024 * 1024)
    rows = pl.pallas_call(
        edges_kernel,
        out_shape=jax.ShapeDtypeStruct((VARS * height + EDGE_ROWS, LANES), f32),
        in_specs=[vmem()],
        out_specs=vmem(),
        compiler_params=grant,
        name="edges",
    )(dq_old)
    cols = pl.pallas_call(
        columns_kernel,
        out_shape=jax.ShapeDtypeStruct((16, height), f32),
        in_specs=[vmem()],
        out_specs=vmem(),
        compiler_params=grant,
        name="columns",
    )(dq_old)
    far = lax.ppermute(rows, "passage", [(q, q ^ 2) for q in range(4)])
    cols = lax.ppermute(cols, "span", [(0, 1), (1, 0)])
    steps = 4
    packed = pl.pallas_call(
        pack_kernel,
        out_shape=jax.ShapeDtypeStruct((blocks, SENT, PART, LANES), f32),
        grid=(steps,),
        in_specs=[
            pl.BlockSpec((VARS, VARS, PLANES, height // steps, LANES), lambda i: (0, 0, 0, i, 0))
        ],
        out_specs=pl.BlockSpec((blocks // steps, SOURCE, PART, LANES), lambda i: (i, 0, 0, 0)),
        compiler_params=grant,
        name="pack",
    )(diag_inverse)
    core = lax.ppermute(rows, "passage", [(q, q ^ 1) for q in range(4)])
    local = pl.pallas_call(
        local_kernel,
        out_shape=jax.ShapeDtypeStruct((VARS, PLANES, height, LANES), f32),
        in_specs=[vmem()] * 4,
        out_specs=vmem(),
        compiler_params=grant,
        name="local",
    )(dq_old, residual, lateral_coef, core)
    cross = lax.ppermute(far, "passage", [(q, q ^ 1) for q in range(4)])
    sent = pl.pallas_call(
        source_kernel,
        out_shape=jax.ShapeDtypeStruct((blocks, SENT, PART, LANES), f32),
        in_specs=[pl.BlockSpec(memory_space=pltpu.SMEM)] + [vmem()] * 9,
        out_specs=vmem(),
        scratch_shapes=[
            pltpu.VMEM((VARS, 2 * height + 8, LANES), f32),
        ],
        input_output_aliases={9: 0},
        compiler_params=grant,
        name="source",
    )(match_list, dq_old, local, lateral_coef, slide_weight[None], core, far, cross, cols, packed)
    got = lax.all_to_all(sent, "stream", 0, 0)
    swept = pl.pallas_call(
        sweep_kernel,
        out_shape=jax.ShapeDtypeStruct((blocks, PLANES * VARS, PART, LANES), f32),
        in_specs=[vmem()],
        out_specs=vmem(),
        compiler_params=grant,
        name="sweep",
    )(got)
    back = lax.all_to_all(swept, "stream", 0, 0)
    return pl.pallas_call(
        unpack_kernel,
        out_shape=jax.ShapeDtypeStruct((VARS, PLANES, height, LANES), f32),
        in_specs=[vmem()],
        out_specs=pl.BlockSpec(memory_space=pltpu.HBM),
        scratch_shapes=[
            pltpu.VMEM((VARS, PLANES, height, LANES), f32),
            pltpu.SemaphoreType.DMA((VARS,)),
        ],
        compiler_params=grant,
        name="unpack",
    )(back)


def solution(mesh):
    placed = (
        P(None, "stream", "passage", "span"),
        P(None, "stream", "passage", "span"),
        P("stream", "passage", "span"),
        P(None, None, "stream", "passage", "span"),
        P("stream", "passage"),
        P("passage"),
    )
    return jax.shard_map(
        on_device,
        mesh=mesh,
        in_specs=placed,
        out_specs=P(None, "stream", "passage", "span"),
        check_vma=False,
    )
```

```python
import jax
import jax.numpy as jnp
from jax import lax
from jax.experimental import pallas as pl
from jax.experimental.pallas import tpu as pltpu
from jax.sharding import PartitionSpec as P

VARS = 6
PAIRS = [(a, b) for a in range(VARS) for b in range(a + 1, VARS)]
COEFS = VARS + len(PAIRS)
PLANES = 2
FORM = PLANES * COEFS
SOURCE = FORM + 1
TERM = SOURCE + PLANES * VARS
SENT = TERM + VARS
LANES = 128
PART = 4
EDGE_ROWS = 16


def vmem():
    return pl.BlockSpec(memory_space=pltpu.VMEM)


def edges_kernel(dq_ref, rows_ref):
    height = dq_ref.shape[2]
    for v in range(VARS):
        rows_ref[height * v : height * (v + 1)] = dq_ref[v, 1]
    edge = height * VARS
    rows_ref[edge:] = jnp.zeros((EDGE_ROWS, LANES), jnp.float32)
    for v in range(VARS):
        rows_ref[edge + 2 * v : edge + 2 * v + 1] = dq_ref[v, 0, 0:1]
        rows_ref[edge + 2 * v + 1 : edge + 2 * v + 2] = dq_ref[v, 0, height - 1 : height]


def columns_kernel(dq_ref, cols_ref):
    span = lax.axis_index("span")
    height = dq_ref.shape[2]
    lane = lax.broadcasted_iota(jnp.int32, (height, LANES), 1)
    cols = jnp.zeros((height, LANES), jnp.float32)
    for i in range(VARS * PLANES):
        shift = i + 2 - 2 * span
        plane = dq_ref[i // PLANES, i % PLANES]
        cols = jnp.where(lane == i + 1 - span, pltpu.roll(plane, shift, 1), cols)
    cols_ref[...] = cols.T[0:16]


def pack_kernel(d_ref, out_ref):
    def put(t, index, value):
        out_ref[2 * t, index] = value[0:PART]
        out_ref[2 * t + 1, index] = value[PART:8]

    for t in range(d_ref.shape[3] // 8):
        blocks = [
            [[d_ref[a, b, p, 8 * t : 8 * t + 8] for b in range(VARS)] for a in range(VARS)]
            for p in range(PLANES)
        ]
        off_row = off_none = off_col = jnp.zeros((8, LANES), jnp.float32)
        for d in blocks:
            for a, b in PAIRS:
                off_row += jnp.abs(d[a][b] * d[b][b] + d[b][a] * d[a][a])
                off_none += jnp.abs(d[a][b] + d[b][a])
                off_col += jnp.abs(d[a][b] * d[a][a] + d[b][a] * d[b][b])
        is_row = (off_row <= off_none) & (off_row <= off_col)
        is_none = off_none <= off_col
        put(t, FORM, jnp.where(is_row, 0.0, jnp.where(is_none, 1.0, 2.0)))
        for p, d in enumerate(blocks):
            s = [d[a][a] for a in range(VARS)]
            size = [jnp.abs(x) for x in s]
            inv = [jnp.where(x == 0.0, 0.0, 1.0 / x) for x in s]
            for a in range(VARS):
                put(t, p * COEFS + a, s[a])
            for i, (a, b) in enumerate(PAIRS):
                larger = size[a] >= size[b]
                row = jnp.where(larger, d[a][b] * inv[a], -d[b][a] * inv[b])
                col = jnp.where(larger, -d[b][a] * inv[a], d[a][b] * inv[b])
                value = jnp.where(is_row, row, jnp.where(is_none, d[a][b], col))
                put(t, p * COEFS + VARS + i, value)


def local_kernel(dq_ref, res_ref, coef_ref, core_ref, out_ref):
    odd = lax.rem(lax.axis_index("passage"), 2) == 1
    height = dq_ref.shape[2]
    sub = lax.broadcasted_iota(jnp.int32, (height, LANES), 0)
    lane = lax.broadcasted_iota(jnp.int32, (height, LANES), 1)
    for v in range(VARS):
        for p in range(PLANES):
            x = dq_ref[v, p]
            last, first = edge_rows(v, p, height)
            above = jnp.where(odd, core_ref[last : last + 1], 0.0)
            below = jnp.where(odd, 0.0, core_ref[first : first + 1])
            up = jnp.where(sub == 0, above, pltpu.roll(x, 1, 0))
            down = jnp.where(sub == height - 1, below, pltpu.roll(x, height - 1, 0))
            left = jnp.where(lane == 0, 0.0, pltpu.roll(x, 1, 1))
            right = jnp.where(lane == LANES - 1, 0.0, pltpu.roll(x, LANES - 1, 1))
            out_ref[v, p] = res_ref[v, p] - coef_ref[p] * (up + down + (left + right))


def edge_rows(v, plane, height):
    if plane:
        return height * (v + 1) - 1, height * v
    return height * VARS + 2 * v + 1, height * VARS + 2 * v


def donors_of(match_ref):
    q = lax.axis_index("passage")
    first = match_ref[...].astype(jnp.float32)[0:1, 0:1]
    start = lax.rem(jnp.max(first).astype(jnp.int32) + 64, 256)
    tile = start // 64
    return jnp.bitwise_xor(tile, q), jnp.bitwise_xor(lax.rem(tile + 1, 4), q), lax.rem(start, 64)


def middle_kernel(
    match_ref, dq_ref, local_ref, coef_ref, weight_ref, core_ref, far_ref, cols_ref, _, out_ref, ring_ref, spread_ref
):
    span = lax.axis_index("span")
    height = dq_ref.shape[2]
    lane = lax.broadcasted_iota(jnp.int32, (height, LANES), 1)
    edge = lane == jnp.where(span == 0, LANES - 1, 0)
    spread_ref[...] = jnp.broadcast_to(weight_ref[...], (LANES, height)).T
    cols = jnp.concatenate([cols_ref[...], jnp.zeros((LANES - 16, height), jnp.float32)], 0).T
    for v in range(VARS):
        for p in range(PLANES):
            side = pltpu.roll(cols, LANES - 1 - (v * PLANES + p), 1)
            value = local_ref[v, p] - coef_ref[p] * jnp.where(edge, side, 0.0)
            for t in range(height // PART):
                out_ref[t, SOURCE + p * VARS + v] = value[PART * t : PART * t + PART]
    ways = donors_of(match_ref)
    for v in range(VARS):
        face = slice(height * v, height * (v + 1))
        for n in range(2):
            near = jnp.where(ways[n] == 0, dq_ref[v, 1], core_ref[face])
            ring_ref[v, height * n : height * (n + 1)] = jnp.where(ways[n] < 2, near, far_ref[face])


def source_kernel(match_ref, coef_ref, cross_ref, near_ref, spread_ref, _, out_ref, ring):
    height = coef_ref.shape[1]
    odd = lax.rem(lax.axis_index("passage"), 2) == 1
    sub = lax.broadcasted_iota(jnp.int32, (PART, LANES), 0)
    beyond = sub == jnp.where(odd, PART - 1, 0)
    part = jnp.where(odd, height // PART - 1, 0)
    ways = donors_of(match_ref)
    for v in range(VARS):
        face = slice(height * v, height * (v + 1))
        for n in range(2):
            rows = slice(height * n, height * (n + 1))
            ring[v, rows] = jnp.where(ways[n] == 3, cross_ref[face], near_ref[v, rows])
        for p in range(PLANES):
            last, first = edge_rows(v, p, height)
            row = jnp.where(odd, cross_ref[first : first + 1], cross_ref[last : last + 1])
            coef = jnp.where(odd, coef_ref[p, height - PART :], coef_ref[p, 0:PART])
            index = SOURCE + p * VARS + v
            out_ref[part, index] = out_ref[part, index] - coef * jnp.where(beyond, row, 0.0)
    for v in range(VARS):
        here = ring[v, pl.ds(ways[2], height)]
        after = ring[v, pl.ds(ways[2] + 1, height)]
        term = (1.0 - spread_ref[...]) * here + spread_ref[...] * after
        for t in range(height // PART):
            out_ref[t, TERM + v] = term[PART * t : PART * t + PART]


def sweep_kernel(in_ref, out_ref):
    blocks = in_ref.shape[0]

    def block_of(b, p):
        base = p * COEFS
        s = [in_ref[b, base + a] for a in range(VARS)]
        k = {pair: in_ref[b, base + VARS + i] for i, pair in enumerate(PAIRS)}
        form = in_ref[b, FORM]
        is_row, is_col = form == 0.0, form == 2.0
        rows = [jnp.where(is_row, x, 1.0) for x in s]
        columns = [jnp.where(is_col, x, 1.0) for x in s]
        return s, k, rows, columns

    def apply(block, x):
        s, k, rows, columns = block
        g = [columns[b] * x[b] for b in range(VARS)]
        out = []
        for a in range(VARS):
            plus = tree([k[a, b] * g[b] for b in range(a + 1, VARS)])
            minus = tree([k[b, a] * g[b] for b in range(a)])
            rest = minus if plus is None else plus if minus is None else plus - minus
            out.append(s[a] * x[a] + rows[a] * (-rest if plus is None else rest))
        return out

    def tree(terms):
        while len(terms) > 1:
            terms = [sum(terms[i : i + 2][1:], terms[i]) for i in range(0, len(terms), 2)]
        return terms[0] if terms else None

    def lower(b, x):
        before = lax.rem(b + blocks - 1, blocks)
        for p in range(PLANES):
            given = [in_ref[b, SOURCE + p * VARS + v] for v in range(VARS)]
            if p == 0:
                given = [given[v] + in_ref[before, TERM + v] for v in range(VARS)]
            x = apply(block_of(b, p), [given[v] + x[v] for v in range(VARS)])
            for v in range(VARS):
                out_ref[b, v * PLANES + p] = x[v]
        return x

    def upper(i, x):
        b = blocks - 1 - i
        for p in reversed(range(PLANES)):
            y = apply(block_of(b, p), x)
            x = [out_ref[b, v * PLANES + p] + y[v] for v in range(VARS)]
            for v in range(VARS):
                out_ref[b, v * PLANES + p] = x[v]
        return x

    zero = [jnp.zeros((PART, LANES), jnp.float32) for _ in range(VARS)]
    lax.fori_loop(0, blocks, lower, zero, unroll=16)
    lax.fori_loop(0, blocks, upper, zero, unroll=16)


def unpack_kernel(in_ref, out_ref, held, sems):
    copies = []
    for v in range(VARS):
        for p in range(PLANES):
            for t in range(in_ref.shape[0]):
                held[v, p, PART * t : PART * t + PART] = in_ref[t, v * PLANES + p]
        copies.append(pltpu.make_async_copy(held.at[v], out_ref.at[v], sems.at[v]))
        copies[v].start()
    for copy in copies:
        copy.wait()


def on_device(residual, dq_old, lateral_coef, diag_inverse, match_list, slide_weight):
    height = residual.shape[2]
    blocks = lax.axis_size("stream")
    f32 = jnp.float32
    grant = pltpu.CompilerParams(vmem_limit_bytes=24 * 1024 * 1024)
    rows = pl.pallas_call(
        edges_kernel,
        out_shape=jax.ShapeDtypeStruct((VARS * height + EDGE_ROWS, LANES), f32),
        in_specs=[vmem()],
        out_specs=vmem(),
        compiler_params=grant,
        name="edges",
    )(dq_old)
    cols = pl.pallas_call(
        columns_kernel,
        out_shape=jax.ShapeDtypeStruct((16, height), f32),
        in_specs=[vmem()],
        out_specs=vmem(),
        compiler_params=grant,
        name="columns",
    )(dq_old)
    far = lax.ppermute(rows, "passage", [(q, q ^ 2) for q in range(4)])
    cols = lax.ppermute(cols, "span", [(0, 1), (1, 0)])
    steps = 4
    packed = pl.pallas_call(
        pack_kernel,
        out_shape=jax.ShapeDtypeStruct((blocks, SENT, PART, LANES), f32),
        grid=(steps,),
        in_specs=[
            pl.BlockSpec((VARS, VARS, PLANES, height // steps, LANES), lambda i: (0, 0, 0, i, 0))
        ],
        out_specs=pl.BlockSpec((blocks // steps, SOURCE, PART, LANES), lambda i: (i, 0, 0, 0)),
        compiler_params=grant,
        name="pack",
    )(diag_inverse)
    core = lax.ppermute(rows, "passage", [(q, q ^ 1) for q in range(4)])
    local = pl.pallas_call(
        local_kernel,
        out_shape=jax.ShapeDtypeStruct((VARS, PLANES, height, LANES), f32),
        in_specs=[vmem()] * 4,
        out_specs=vmem(),
        compiler_params=grant,
        name="local",
    )(dq_old, residual, lateral_coef, core)
    cross = lax.ppermute(far, "passage", [(q, q ^ 1) for q in range(4)])
    whole = jax.ShapeDtypeStruct((blocks, SENT, PART, LANES), f32)
    sent, near, spread = pl.pallas_call(
        middle_kernel,
        out_shape=(
            whole,
            jax.ShapeDtypeStruct((VARS, 2 * height, LANES), f32),
            jax.ShapeDtypeStruct((height, LANES), f32),
        ),
        in_specs=[vmem()] * 9,
        out_specs=(vmem(), vmem(), vmem()),
        input_output_aliases={8: 0},
        compiler_params=grant,
        name="middle",
    )(match_list, dq_old, local, lateral_coef, slide_weight[None], core, far, cols, packed)
    sent = pl.pallas_call(
        source_kernel,
        out_shape=whole,
        in_specs=[vmem()] * 6,
        out_specs=vmem(),
        scratch_shapes=[pltpu.VMEM((VARS, 2 * height + 8, LANES), f32)],
        input_output_aliases={5: 0},
        compiler_params=grant,
        name="source",
    )(match_list, lateral_coef, cross, near, spread, sent)
    got = lax.all_to_all(sent, "stream", 0, 0)
    swept = pl.pallas_call(
        sweep_kernel,
        out_shape=jax.ShapeDtypeStruct((blocks, PLANES * VARS, PART, LANES), f32),
        in_specs=[vmem()],
        out_specs=vmem(),
        compiler_params=grant,
        name="sweep",
    )(got)
    back = lax.all_to_all(swept, "stream", 0, 0)
    return pl.pallas_call(
        unpack_kernel,
        out_shape=jax.ShapeDtypeStruct((VARS, PLANES, height, LANES), f32),
        in_specs=[vmem()],
        out_specs=pl.BlockSpec(memory_space=pltpu.HBM),
        scratch_shapes=[
            pltpu.VMEM((VARS, PLANES, height, LANES), f32),
            pltpu.SemaphoreType.DMA((VARS,)),
        ],
        compiler_params=grant,
        name="unpack",
    )(back)


def solution(mesh):
    placed = (
        P(None, "stream", "passage", "span"),
        P(None, "stream", "passage", "span"),
        P("stream", "passage", "span"),
        P(None, None, "stream", "passage", "span"),
        P("stream", "passage"),
        P("passage"),
    )
    return jax.shard_map(
        on_device,
        mesh=mesh,
        in_specs=placed,
        out_specs=P(None, "stream", "passage", "span"),
        check_vma=False,
    )
```

```python
import functools

import jax
import jax.numpy as jnp
from jax import lax
from jax.experimental import pallas as pl
from jax.experimental.pallas import tpu as pltpu
from jax.sharding import PartitionSpec as P

VARS = 6
PAIRS = [(a, b) for a in range(VARS) for b in range(a + 1, VARS)]
COEFS = VARS + len(PAIRS)
PLANES = 2
FORM = PLANES * COEFS
SOURCE = FORM + 1
TERM = SOURCE + PLANES * VARS
SENT = TERM + VARS
LANES = 128
PART = 4
EDGE_ROWS = 16


def vmem():
    return pl.BlockSpec(memory_space=pltpu.VMEM)


def edges_kernel(dq_ref, rows_ref):
    height = dq_ref.shape[2]
    for v in range(VARS):
        rows_ref[height * v : height * (v + 1)] = dq_ref[v, 1]
    edge = height * VARS
    rows_ref[edge:] = jnp.zeros((EDGE_ROWS, LANES), jnp.float32)
    for v in range(VARS):
        rows_ref[edge + 2 * v : edge + 2 * v + 1] = dq_ref[v, 0, 0:1]
        rows_ref[edge + 2 * v + 1 : edge + 2 * v + 2] = dq_ref[v, 0, height - 1 : height]


def columns_kernel(dq_ref, cols_ref):
    span = lax.axis_index("span")
    height = dq_ref.shape[2]
    lane = lax.broadcasted_iota(jnp.int32, (height, LANES), 1)
    cols = jnp.zeros((height, LANES), jnp.float32)
    for i in range(VARS * PLANES):
        shift = i + 2 - 2 * span
        plane = dq_ref[i // PLANES, i % PLANES]
        cols = jnp.where(lane == i + 1 - span, pltpu.roll(plane, shift, 1), cols)
    cols_ref[...] = cols.T[0:16]


def pack_kernel(d_ref, out_ref):
    def put(t, index, value):
        out_ref[2 * t, index] = value[0:PART]
        out_ref[2 * t + 1, index] = value[PART:8]

    for t in range(d_ref.shape[3] // 8):
        blocks = [
            [[d_ref[a, b, p, 8 * t : 8 * t + 8] for b in range(VARS)] for a in range(VARS)]
            for p in range(PLANES)
        ]
        off_row = off_none = off_col = jnp.zeros((8, LANES), jnp.float32)
        for d in blocks:
            for a, b in PAIRS:
                off_row += jnp.abs(d[a][b] * d[b][b] + d[b][a] * d[a][a])
                off_none += jnp.abs(d[a][b] + d[b][a])
                off_col += jnp.abs(d[a][b] * d[a][a] + d[b][a] * d[b][b])
        is_row = (off_row <= off_none) & (off_row <= off_col)
        is_none = off_none <= off_col
        put(t, FORM, jnp.where(is_row, 0.0, jnp.where(is_none, 1.0, 2.0)))
        for p, d in enumerate(blocks):
            s = [d[a][a] for a in range(VARS)]
            size = [jnp.abs(x) for x in s]
            inv = [jnp.where(x == 0.0, 0.0, 1.0 / x) for x in s]
            for a in range(VARS):
                put(t, p * COEFS + a, s[a])
            for i, (a, b) in enumerate(PAIRS):
                larger = size[a] >= size[b]
                row = jnp.where(larger, d[a][b] * inv[a], -d[b][a] * inv[b])
                col = jnp.where(larger, -d[b][a] * inv[a], d[a][b] * inv[b])
                value = jnp.where(is_row, row, jnp.where(is_none, d[a][b], col))
                put(t, p * COEFS + VARS + i, value)


def local_kernel(dq_ref, res_ref, coef_ref, core_ref, out_ref):
    odd = lax.rem(lax.axis_index("passage"), 2) == 1
    height = dq_ref.shape[2]
    sub = lax.broadcasted_iota(jnp.int32, (height, LANES), 0)
    lane = lax.broadcasted_iota(jnp.int32, (height, LANES), 1)
    for v in range(VARS):
        for p in range(PLANES):
            x = dq_ref[v, p]
            last, first = edge_rows(v, p, height)
            above = jnp.where(odd, core_ref[last : last + 1], 0.0)
            below = jnp.where(odd, 0.0, core_ref[first : first + 1])
            up = jnp.where(sub == 0, above, pltpu.roll(x, 1, 0))
            down = jnp.where(sub == height - 1, below, pltpu.roll(x, height - 1, 0))
            left = jnp.where(lane == 0, 0.0, pltpu.roll(x, 1, 1))
            right = jnp.where(lane == LANES - 1, 0.0, pltpu.roll(x, LANES - 1, 1))
            out_ref[v, p] = res_ref[v, p] - coef_ref[p] * (up + down + (left + right))


def edge_rows(v, plane, height):
    if plane:
        return height * (v + 1) - 1, height * v
    return height * VARS + 2 * v + 1, height * VARS + 2 * v


def donors_of(match_ref):
    q = lax.axis_index("passage")
    first = match_ref[...].astype(jnp.float32)[0:1, 0:1]
    start = lax.rem(jnp.max(first).astype(jnp.int32) + 64, 256)
    tile = start // 64
    return jnp.bitwise_xor(tile, q), jnp.bitwise_xor(lax.rem(tile + 1, 4), q), lax.rem(start, 64)


def middle_kernel(
    match_ref, dq_ref, local_ref, coef_ref, weight_ref, core_ref, far_ref, cols_ref, _, out_ref, ring_ref, spread_ref
):
    span = lax.axis_index("span")
    height = dq_ref.shape[2]
    lane = lax.broadcasted_iota(jnp.int32, (height, LANES), 1)
    edge = lane == jnp.where(span == 0, LANES - 1, 0)
    spread_ref[...] = jnp.broadcast_to(weight_ref[...], (LANES, height)).T
    cols = jnp.concatenate([cols_ref[...], jnp.zeros((LANES - 16, height), jnp.float32)], 0).T
    for v in range(VARS):
        for p in range(PLANES):
            side = pltpu.roll(cols, LANES - 1 - (v * PLANES + p), 1)
            value = local_ref[v, p] - coef_ref[p] * jnp.where(edge, side, 0.0)
            for t in range(height // PART):
                out_ref[t, SOURCE + p * VARS + v] = value[PART * t : PART * t + PART]
    ways = donors_of(match_ref)
    for v in range(VARS):
        face = slice(height * v, height * (v + 1))
        for n in range(2):
            near = jnp.where(ways[n] == 0, dq_ref[v, 1], core_ref[face])
            ring_ref[v, height * n : height * (n + 1)] = jnp.where(ways[n] < 2, near, far_ref[face])


def source_kernel(match_ref, coef_ref, cross_ref, near_ref, spread_ref, _, out_ref, ring):
    height = coef_ref.shape[1]
    odd = lax.rem(lax.axis_index("passage"), 2) == 1
    sub = lax.broadcasted_iota(jnp.int32, (PART, LANES), 0)
    beyond = sub == jnp.where(odd, PART - 1, 0)
    part = jnp.where(odd, height // PART - 1, 0)
    ways = donors_of(match_ref)
    for v in range(VARS):
        face = slice(height * v, height * (v + 1))
        for n in range(2):
            rows = slice(height * n, height * (n + 1))
            ring[v, rows] = jnp.where(ways[n] == 3, cross_ref[face], near_ref[v, rows])
        for p in range(PLANES):
            last, first = edge_rows(v, p, height)
            row = jnp.where(odd, cross_ref[first : first + 1], cross_ref[last : last + 1])
            coef = jnp.where(odd, coef_ref[p, height - PART :], coef_ref[p, 0:PART])
            index = SOURCE + p * VARS + v
            out_ref[part, index] = out_ref[part, index] - coef * jnp.where(beyond, row, 0.0)
    for v in range(VARS):
        here = ring[v, pl.ds(ways[2], height)]
        after = ring[v, pl.ds(ways[2] + 1, height)]
        term = (1.0 - spread_ref[...]) * here + spread_ref[...] * after
        for t in range(height // PART):
            out_ref[t, TERM + v] = term[PART * t : PART * t + PART]


def sweep_kernel(in_ref, out_ref):
    blocks = in_ref.shape[0]

    def block_of(b, p):
        base = p * COEFS
        s = [in_ref[b, base + a] for a in range(VARS)]
        k = {pair: in_ref[b, base + VARS + i] for i, pair in enumerate(PAIRS)}
        return s, k, in_ref[b, FORM]

    def apply(block, x, general):
        s, k, form = block
        g = [jnp.where(form == 2.0, s[b], 1.0) * x[b] for b in range(VARS)] if general else x
        out = []
        for a in range(VARS):
            plus = tree([k[a, b] * g[b] for b in range(a + 1, VARS)])
            minus = tree([k[b, a] * g[b] for b in range(a)])
            rest = minus if plus is None else plus if minus is None else plus - minus
            rest = -rest if plus is None else rest
            if general:
                out.append(s[a] * x[a] + jnp.where(form == 0.0, s[a], 1.0) * rest)
            else:
                out.append(s[a] * (x[a] + rest))
        return out

    def tree(terms):
        while len(terms) > 1:
            terms = [sum(terms[i : i + 2][1:], terms[i]) for i in range(0, len(terms), 2)]
        return terms[0] if terms else None

    def lower(general, b, x):
        before = lax.rem(b + blocks - 1, blocks)
        for p in range(PLANES):
            given = [in_ref[b, SOURCE + p * VARS + v] for v in range(VARS)]
            if p == 0:
                given = [given[v] + in_ref[before, TERM + v] for v in range(VARS)]
            x = apply(block_of(b, p), [given[v] + x[v] for v in range(VARS)], general)
            for v in range(VARS):
                out_ref[b, v * PLANES + p] = x[v]
        return x

    def upper(general, i, x):
        b = blocks - 1 - i
        for p in reversed(range(PLANES)):
            y = apply(block_of(b, p), x, general)
            x = [out_ref[b, v * PLANES + p] + y[v] for v in range(VARS)]
            for v in range(VARS):
                out_ref[b, v * PLANES + p] = x[v]
        return x

    def sweep(general):
        zero = [jnp.zeros((PART, LANES), jnp.float32) for _ in range(VARS)]
        lax.fori_loop(0, blocks, functools.partial(lower, general), zero, unroll=blocks)
        lax.fori_loop(0, blocks, functools.partial(upper, general), zero, unroll=blocks)

    form = in_ref[0, FORM]
    for b in range(1, blocks):
        form = jnp.maximum(form, in_ref[b, FORM])
    scaled = jnp.max(form) == 0.0
    pl.when(scaled)(lambda: sweep(False))
    pl.when(jnp.logical_not(scaled))(lambda: sweep(True))


def unpack_kernel(in_ref, out_ref, held, sems):
    copies = []
    for v in range(VARS):
        for p in range(PLANES):
            for t in range(in_ref.shape[0]):
                held[v, p, PART * t : PART * t + PART] = in_ref[t, v * PLANES + p]
        copies.append(pltpu.make_async_copy(held.at[v], out_ref.at[v], sems.at[v]))
        copies[v].start()
    for copy in copies:
        copy.wait()


def on_device(residual, dq_old, lateral_coef, diag_inverse, match_list, slide_weight):
    height = residual.shape[2]
    blocks = lax.axis_size("stream")
    f32 = jnp.float32
    grant = pltpu.CompilerParams(vmem_limit_bytes=24 * 1024 * 1024)
    rows = pl.pallas_call(
        edges_kernel,
        out_shape=jax.ShapeDtypeStruct((VARS * height + EDGE_ROWS, LANES), f32),
        in_specs=[vmem()],
        out_specs=vmem(),
        compiler_params=grant,
        name="edges",
    )(dq_old)
    cols = pl.pallas_call(
        columns_kernel,
        out_shape=jax.ShapeDtypeStruct((16, height), f32),
        in_specs=[vmem()],
        out_specs=vmem(),
        compiler_params=grant,
        name="columns",
    )(dq_old)
    far = lax.ppermute(rows, "passage", [(q, q ^ 2) for q in range(4)])
    cols = lax.ppermute(cols, "span", [(0, 1), (1, 0)])
    steps = 4
    packed = pl.pallas_call(
        pack_kernel,
        out_shape=jax.ShapeDtypeStruct((blocks, SENT, PART, LANES), f32),
        grid=(steps,),
        in_specs=[
            pl.BlockSpec((VARS, VARS, PLANES, height // steps, LANES), lambda i: (0, 0, 0, i, 0))
        ],
        out_specs=pl.BlockSpec((blocks // steps, SOURCE, PART, LANES), lambda i: (i, 0, 0, 0)),
        compiler_params=grant,
        name="pack",
    )(diag_inverse)
    core = lax.ppermute(rows, "passage", [(q, q ^ 1) for q in range(4)])
    local = pl.pallas_call(
        local_kernel,
        out_shape=jax.ShapeDtypeStruct((VARS, PLANES, height, LANES), f32),
        in_specs=[vmem()] * 4,
        out_specs=vmem(),
        compiler_params=grant,
        name="local",
    )(dq_old, residual, lateral_coef, core)
    cross = lax.ppermute(far, "passage", [(q, q ^ 1) for q in range(4)])
    whole = jax.ShapeDtypeStruct((blocks, SENT, PART, LANES), f32)
    sent, near, spread = pl.pallas_call(
        middle_kernel,
        out_shape=(
            whole,
            jax.ShapeDtypeStruct((VARS, 2 * height, LANES), f32),
            jax.ShapeDtypeStruct((height, LANES), f32),
        ),
        in_specs=[vmem()] * 9,
        out_specs=(vmem(), vmem(), vmem()),
        input_output_aliases={8: 0},
        compiler_params=grant,
        name="middle",
    )(match_list, dq_old, local, lateral_coef, slide_weight[None], core, far, cols, packed)
    sent = pl.pallas_call(
        source_kernel,
        out_shape=whole,
        in_specs=[vmem()] * 6,
        out_specs=vmem(),
        scratch_shapes=[pltpu.VMEM((VARS, 2 * height + 8, LANES), f32)],
        input_output_aliases={5: 0},
        compiler_params=grant,
        name="source",
    )(match_list, lateral_coef, cross, near, spread, sent)
    got = lax.all_to_all(sent, "stream", 0, 0)
    swept = pl.pallas_call(
        sweep_kernel,
        out_shape=jax.ShapeDtypeStruct((blocks, PLANES * VARS, PART, LANES), f32),
        in_specs=[vmem()],
        out_specs=vmem(),
        compiler_params=pltpu.CompilerParams(vmem_limit_bytes=24 * 1024 * 1024),
        name="sweep",
    )(got)
    back = lax.all_to_all(swept, "stream", 0, 0)
    return pl.pallas_call(
        unpack_kernel,
        out_shape=jax.ShapeDtypeStruct((VARS, PLANES, height, LANES), f32),
        in_specs=[vmem()],
        out_specs=pl.BlockSpec(memory_space=pltpu.HBM),
        scratch_shapes=[
            pltpu.VMEM((VARS, PLANES, height, LANES), f32),
            pltpu.SemaphoreType.DMA((VARS,)),
        ],
        compiler_params=grant,
        name="unpack",
    )(back)


def solution(mesh):
    placed = (
        P(None, "stream", "passage", "span"),
        P(None, "stream", "passage", "span"),
        P("stream", "passage", "span"),
        P(None, None, "stream", "passage", "span"),
        P("stream", "passage"),
        P("passage"),
    )
    return jax.shard_map(
        on_device,
        mesh=mesh,
        in_specs=placed,
        out_specs=P(None, "stream", "passage", "span"),
        check_vma=False,
    )
```
